512 devices in a mesh: row: 32 (over x, z_lo, core), col: 16 (over y, z_hi).
Axes of the slice: x: 4, y: 4, z: 16 (z_hi: 4, z_lo: 4; z = z_hi * 4 + z_lo), core: 2. Of those that a mesh axis runs over, the one named last changes fastest.
Arguments:
- features: bfloat16 [65536, 128], P(('row', 'col')), may hold values from -6 to 6
- weight: bfloat16 [128, 128], replicated, may hold values from -0.5 to 0.5
- adj_values: bfloat16 [32, 16, 16, 128, 128], P('row', 'col'), may hold values from -0.125 to 0.125
- tile_rows: int32 [32, 16, 16], P('row', 'col'), may hold values from 0 to 15
- tile_cols: int32 [32, 16, 16], P('row', 'col'), may hold values from 0 to 31
- cotangent: bfloat16 [65536, 128], P(('row', 'col')), may hold values from -6 to 6
Outputs:
- activations: float32 [65536, 128], P(('row', 'col'))
- grad_features: float32 [65536, 128], P(('row', 'col'))
- grad_weight: float32 [128, 128], replicated
The draws below stay inside these ranges and needn't reach their ends.
All inputs are finite; a program needn't handle non-finite values.
Results may differ from the reference program's by a relative error of at most 0.0049.
Values may be sent and summed in bfloat16 or wider, within the bound.
No kernel may reach another device: no remote copies, remote signals or barrier semaphores. Data moves between devices by JAX's collectives and lax.ppermute only.
A program may use at most 64 MiB of HBM per device.

```python
import math
import jax
import jax.numpy as jnp
import numpy as np
from jax import lax

F = 128
TILE = 128
RD = 128
NT = 16
N = 65536
TR = 16
TC = 32
N_ROW = 32
N_COL = 16


def with_ends(result, stream_key, least, largest):
    longest = result.shape.index(max(result.shape))
    spots = []
    for shift in (0, 1):
        where = [jax.random.randint(jax.random.fold_in(stream_key, axis), (), 0, length) for axis, length in enumerate(result.shape)]
        where[longest] = (where[longest] + shift) % result.shape[longest]
        spots.append(tuple(where))
    return result.at[spots[0]].set(least).at[spots[1]].set(largest)


def steps_of(stream_key, shape, shards, smallest, top_value):
    level, own = 1.0, jax.random.fold_in(stream_key, 6)
    for axis_at, shards_of in shards:
        draws = jnp.exp(jax.random.uniform(jax.random.fold_in(own, axis_at), (shards_of,), jnp.float32, smallest / len(shards), top_value / len(shards)))
        level = level * jnp.repeat(draws, shape[axis_at] // shards_of).reshape([-1 if axis == axis_at else 1 for axis in range(len(shape))])
    return level


def rank_table(count, slope):
    loads = [(1 << 20) // math.isqrt(standing ** slope) + 1 for standing in range(1, count + 1)]
    scale = 1 + sum(loads) // (1 << 30)
    return np.cumsum(np.array([max(1, weight // scale) for weight in loads]))


def ranked_ids(key, dims, amount, lean):
    table = rank_table(amount, lean)
    ticket = jax.random.randint(jax.random.fold_in(key, 1), dims, 0, int(table[amount - 1]))
    rank = jnp.searchsorted(jnp.asarray(table, jnp.int32), ticket, side="right")
    return jax.random.permutation(jax.random.fold_in(key, 2), amount)[rank].astype(jnp.int32)


def gaussian(own_key, shape, scale, most, pieces=(), held_as=jnp.bfloat16):
    gain = steps_of(own_key, shape, pieces, -0.22, 0.18) if pieces else 1.0
    values = jax.random.normal(own_key, shape, jnp.float32) * scale * gain
    return jnp.minimum(jnp.maximum(values, -most), most).astype(held_as)


def setup_inputs(seed: int = 0) -> dict:
    seeds = jax.random.split(jax.random.key(seed), 7)
    return {
        "features": gaussian(seeds[0], (N, F), 1.0, 6.0, ((0, 512),)),
        "weight": gaussian(seeds[1], (F, F), F ** -0.5, 0.5),
        "adj_values": gaussian(seeds[2], (N_ROW, N_COL, NT, TILE, TILE), (NT * TILE * TILE // RD) ** -0.5, 0.125, ((0, 32), (1, 16))),
        "tile_rows": with_ends(jax.random.randint(seeds[3], (N_ROW, N_COL, NT), 0, TR), jax.random.fold_in(seeds[3], 1), 0, TR - 1).astype(jnp.int32),
        "tile_cols": with_ends(ranked_ids(seeds[4], (N_ROW, N_COL, NT), TC, 2), jax.random.fold_in(seeds[4], 3), 0, TC - 1).astype(jnp.int32),
        "cotangent": gaussian(seeds[5], (N, F), 1.0, 6.0, ((0, 512),)),
    }


def reference(features, weight, adj_values, tile_rows, tile_cols, cotangent):
    xcols = features.reshape(N_ROW, N_COL, RD, F).transpose(1, 0, 2, 3).reshape(N_COL, TC, TILE, F)

    def forward_block(carry, inputs):
        blocks, rows_id, cols_id = inputs
        picked = jax.vmap(lambda xc, cc: xc[cc])(xcols, cols_id)
        prods = jnp.einsum("jtab,jtbf->jtaf", blocks.astype(jnp.float32), picked.astype(jnp.float32))
        summed = jax.ops.segment_sum(prods.reshape(N_COL * NT, TILE, F), rows_id.reshape(-1), num_segments=TR)
        return carry, summed.reshape(TR * TILE, F)

    _, zblocks = lax.scan(forward_block, jnp.float32(0.0), (adj_values, tile_rows, tile_cols))
    aggregated = zblocks.reshape(N, F)
    zed = aggregated.astype(jnp.bfloat16)
    pre = jnp.dot(zed, weight, preferred_element_type=jnp.float32)
    sig = jax.nn.sigmoid(pre)
    activations = pre * sig
    dpre = (cotangent.astype(jnp.float32) * sig * (1.0 + pre * (1.0 - sig))).astype(jnp.bfloat16)
    grad_weight = jnp.dot(zed.T, dpre, preferred_element_type=jnp.float32)
    dzed = jnp.dot(dpre, weight.T, preferred_element_type=jnp.float32).astype(jnp.bfloat16)
    drows = dzed.reshape(N_ROW, TR, TILE, F)

    def backward_block(carry, inputs):
        blocks, rows_id, cols_id, drow = inputs
        picked = jax.vmap(lambda cc: drow[cc])(rows_id)
        prods = jnp.einsum("jtab,jtaf->jtbf", blocks.astype(jnp.float32), picked.astype(jnp.float32))
        summed = jax.vmap(lambda pp, cc: jax.ops.segment_sum(pp, cc, num_segments=TC))(prods, cols_id)
        return carry + summed, jnp.float32(0.0)

    start = jnp.zeros((N_COL, TC, TILE, F), jnp.float32)
    total, _ = lax.scan(backward_block, start, (adj_values, tile_rows, tile_cols, drows))
    grad_features = total.reshape(N_COL, N_ROW, RD, F).transpose(1, 0, 2, 3).reshape(N, F)
    return activations, grad_features, grad_weight
```

```python
import itertools

import jax
import jax.numpy as jnp
from jax import lax
from jax.experimental import pallas as pl
from jax.experimental.pallas import tpu as pltpu
from jax.sharding import PartitionSpec as P

BOTH = ("row", "col")
SIZES = {"x": 4, "zl": 4, "core": 2, "y": 4, "zh": 4}
F = 128
T = 128
BF = jnp.bfloat16
F32 = jnp.float32


def position(place):
    n = 0
    for name, size in SIZES.items():
        n = n * size + place[name]
    return n


def places():
    for values in itertools.product(*(range(s) for s in SIZES.values())):
        yield dict(zip(SIZES, values))


def groups(axis):
    found = {}
    for place in places():
        key = tuple(v for n, v in place.items() if n != axis)
        found.setdefault(key, []).append(position(place))
    return list(found.values())


def swap_core(array):
    pairs = [(position(p), position({**p, "core": 1 - p["core"]})) for p in places()]
    return lax.ppermute(array, BOTH, pairs)


def gather(array, axis):
    return lax.all_gather(array, BOTH, axis=0, tiled=False, axis_index_groups=groups(axis))


def exchange(array, axis):
    return lax.all_to_all(array, BOTH, 0, 0, tiled=True, axis_index_groups=groups(axis))


def dot(a, b, dims):
    return lax.dot_general(a, b, (dims, ((), ())), preferred_element_type=F32)


def call(body, outs, spaces, scratch=()):
    kinds = {"v": pltpu.VMEM, "s": pltpu.SMEM}
    return pl.pallas_call(
        body,
        out_shape=[jax.ShapeDtypeStruct(s, d) for s, d in outs],
        in_specs=[pl.BlockSpec(memory_space=kinds[k]) for k in spaces],
        out_specs=[pl.BlockSpec(memory_space=pltpu.VMEM) for _ in outs],
        scratch_shapes=list(scratch),
    )


def forward_tiles(rows, cols, adj, own, other, out, acc):
    core = lax.rem(lax.axis_index("row"), 2)
    acc[...] = jnp.zeros_like(acc)
    for t in range(16):
        b = cols[t]
        spot = lax.div(b, 2)
        mine = lax.rem(b, 2) == core
        x = jnp.where(mine, own[spot], other[spot])
        r = rows[t]
        acc[r] += dot(adj[t], x, ((1,), (0,)))
    out[...] = acc[...].astype(BF)


def sum_rows(parts, cot, out):
    total = parts[0].astype(F32)
    for k in range(1, 4):
        total += parts[k].astype(F32)
    out[pl.ds(0, 512), :] = total.astype(BF)
    out[pl.ds(512, 128), :] = cot[...]


def layer(parts, weight, act, out, kept):
    total = parts[0, pl.ds(0, 512), :].astype(F32)
    for k in range(1, 4):
        total += parts[k, pl.ds(0, 512), :].astype(F32)
    zed = total.astype(BF)
    w = weight[...]
    pre = dot(zed, w, ((1,), (0,)))
    sig = jax.nn.sigmoid(pre)
    kept[...] = (pre * sig).reshape(4, T, F)
    act[...] = kept[lax.rem(lax.axis_index("col"), 4)]
    cot = jnp.concatenate([parts[k, pl.ds(512, 128), :] for k in range(4)], axis=0)
    dpre = (cot.astype(F32) * sig * (1.0 + pre * (1.0 - sig))).astype(BF)
    out[pl.ds(0, 512), :] = dot(dpre, w, ((1,), (1,))).astype(BF)
    grad = dot(zed, dpre, ((0,), (0,)))
    high = grad.astype(BF)
    out[pl.ds(512, 128), :] = high
    out[pl.ds(640, 128), :] = (grad - high.astype(F32)).astype(BF)


def backward_tiles(rows, cols, adj, parts, keep, send, acc):
    core = lax.rem(lax.axis_index("row"), 2)
    acc[...] = jnp.zeros_like(acc)
    for t in range(16):
        r = rows[t]
        b = cols[t]
        start = pl.multiple_of(lax.rem(r, 4) * T, T)
        d = parts[lax.div(r, 4), pl.ds(start, T), :]
        acc[lax.rem(b, 2), lax.div(b, 2)] += dot(adj[t], d, ((0,), (0,)))
    keep[pl.ds(0, 16)] = acc[core]
    send[pl.ds(0, 16)] = acc[1 - core]
    grad = jnp.zeros((F, F), F32)
    for k in range(4):
        grad += parts[k, pl.ds(512, 128), :].astype(F32)
        grad += parts[k, pl.ds(640, 128), :].astype(F32)
    keep[16] = grad
    send[16] = grad


def split(grad):
    high = grad.astype(BF)
    return high, (grad - high.astype(F32)).astype(BF)


def add_cores(keep, got, out):
    high, low = split(keep[16] + got[16])
    for k in range(4):
        tiles = keep[pl.ds(4 * k, 4)] + got[pl.ds(4 * k, 4)]
        out[k, pl.ds(0, 4)] = tiles.astype(BF)
        out[k, 4] = high
        out[k, 5] = low


def add_x(parts, out):
    total = parts[0].astype(F32)
    for k in range(1, 4):
        total += parts[k].astype(F32)
    high, low = split(total[4] + total[5])
    for k in range(4):
        out[k, 0] = total[k].astype(BF)
        out[k, 1] = high
        out[k, 2] = low


def add_z(parts, out, grad):
    total = parts[0].astype(F32)
    for k in range(1, 4):
        total += parts[k].astype(F32)
    out[...] = total[0]
    grad[...] = total[1] + total[2]


def per_device(features, weight, adj_values, tile_rows, tile_cols, cotangent):
    adj = adj_values.reshape(16, T, T)
    rows = tile_rows.reshape(16)
    cols = tile_cols.reshape(16)

    own = gather(gather(features, "zl"), "x").reshape(16, T, F)
    other = swap_core(own)
    (partial,) = call(
        forward_tiles, [((16, T, F), BF)], "ssvvv", [pltpu.VMEM((16, T, F), F32)]
    )(rows, cols, adj, own, other)
    parts = exchange(partial.reshape(4, 512, F), "y")
    (summed,) = call(sum_rows, [((640, F), BF)], "vv")(parts, cotangent)
    parts = gather(summed, "zh")
    act, back = call(
        layer, [((T, F), F32), ((768, F), BF)], "vv", [pltpu.VMEM((4, T, F), F32)]
    )(parts, weight)
    parts = gather(back, "y")
    keep, send = call(
        backward_tiles,
        [((17, T, F), F32), ((17, T, F), F32)],
        "ssvv",
        [pltpu.VMEM((2, 16, T, F), F32)],
    )(rows, cols, adj, parts)
    got = swap_core(send)
    (parts,) = call(add_cores, [((4, 6, T, F), BF)], "vv")(keep, got)
    parts = exchange(parts, "x")
    (parts,) = call(add_x, [((4, 3, T, F), BF)], "v")(parts)
    parts = exchange(parts, "zl")
    out, grad = call(add_z, [((T, F), F32), ((F, F), F32)], "v")(parts)
    return act, out, grad


def solution(mesh):
    return jax.shard_map(
        per_device,
        mesh=mesh,
        in_specs=(
            P(BOTH, None),
            P(),
            P("row", "col", None, None, None),
            P("row", "col", None),
            P("row", "col", None),
            P(BOTH, None),
        ),
        out_specs=(P(BOTH, None), P(BOTH, None), P()),
        check_vma=False,
    )
```

```python
import itertools

import jax
import jax.numpy as jnp
from jax import lax
from jax.experimental import pallas as pl
from jax.experimental.pallas import tpu as pltpu
from jax.sharding import PartitionSpec as P

BOTH = ("row", "col")
SIZES = {"x": 4, "zl": 4, "core": 2, "y": 4, "zh": 4}
F = 128
T = 128
BF = jnp.bfloat16
F32 = jnp.float32


def position(place):
    n = 0
    for name, size in SIZES.items():
        n = n * size + place[name]
    return n


def places():
    for values in itertools.product(*(range(s) for s in SIZES.values())):
        yield dict(zip(SIZES, values))


def groups(axis):
    found = {}
    for place in places():
        key = tuple(v for n, v in place.items() if n != axis)
        found.setdefault(key, []).append(position(place))
    return list(found.values())


def swap_core(array):
    pairs = [(position(p), position({**p, "core": 1 - p["core"]})) for p in places()]
    return lax.ppermute(array, BOTH, pairs)


def gather(array, axis):
    return exchange(jnp.broadcast_to(array[None], (4, *array.shape)), axis)


def exchange(array, axis):
    return lax.all_to_all(array, BOTH, 0, 0, tiled=True, axis_index_groups=groups(axis))


def dot(a, b, dims):
    return lax.dot_general(a, b, (dims, ((), ())), preferred_element_type=F32)


def call(body, outs, spaces, scratch=()):
    kinds = {"v": pltpu.VMEM, "s": pltpu.SMEM}
    return pl.pallas_call(
        body,
        out_shape=[jax.ShapeDtypeStruct(s, d) for s, d in outs],
        in_specs=[pl.BlockSpec(memory_space=kinds[k]) for k in spaces],
        out_specs=[pl.BlockSpec(memory_space=pltpu.VMEM) for _ in outs],
        scratch_shapes=list(scratch),
    )


def forward_tiles(rows, cols, adj, own, other, out, mine, acc):
    core = lax.rem(lax.axis_index("row"), 2)
    acc[...] = jnp.zeros_like(acc)
    for t in range(16):
        b = cols[t]
        spot = lax.div(b, 2)
        x = jnp.where(lax.rem(b, 2) == core, own[spot], other[spot])
        r = rows[t]
        acc[r] += dot(adj[t], x, ((1,), (0,)))
    out[...] = acc[...].astype(BF).reshape(4, 4, T, F)
    mine[...] = acc[pl.ds(lax.div(lax.axis_index("col"), 4) * 4, 4)]


def layer(parts, cots, weight, act, out, kept):
    total = parts[0].astype(F32)
    for k in range(1, 4):
        total += parts[k].astype(F32)
    zed = total.reshape(512, F).astype(BF)
    w = weight[...]
    pre = dot(zed, w, ((1,), (0,)))
    sig = jax.nn.sigmoid(pre)
    kept[...] = (pre * sig).reshape(4, T, F)
    act[...] = kept[lax.rem(lax.axis_index("col"), 4)]
    cot = cots[...].reshape(512, F)
    dpre = (cot.astype(F32) * sig * (1.0 + pre * (1.0 - sig))).astype(BF)
    back = dot(dpre, w, ((1,), (1,))).astype(BF).reshape(4, T, F)
    grad = dot(zed, dpre, ((0,), (0,)))
    high, low = split(grad)
    for k in range(4):
        out[k, pl.ds(0, 4)] = back
        out[k, 4] = high
        out[k, 5] = low


def backward_tiles(rows, cols, adj, parts, keep, send, acc):
    core = lax.rem(lax.axis_index("row"), 2)
    acc[...] = jnp.zeros_like(acc)
    for t in range(16):
        r = rows[t]
        b = cols[t]
        d = parts[lax.div(r, 4), lax.rem(r, 4)]
        acc[lax.rem(b, 2), lax.div(b, 2)] += dot(adj[t], d, ((0,), (0,)))
    keep[pl.ds(0, 16)] = acc[core]
    send[pl.ds(0, 16)] = acc[1 - core]
    grad = jnp.zeros((F, F), F32)
    for k in range(4):
        grad += parts[k, 4].astype(F32) + parts[k, 5].astype(F32)
    keep[16] = grad
    send[16] = grad


def split(grad):
    high = grad.astype(BF)
    return high, (grad - high.astype(F32)).astype(BF)


def spread(array):
    return jnp.broadcast_to(array[None], (4, *array.shape))


def add_received(own, parts, place):
    others = jnp.arange(4).reshape(4, 1, 1, 1) != place
    return own + jnp.sum(jnp.where(others, parts.astype(F32), 0.0), axis=0)


def per_device(features, weight, adj_values, tile_rows, tile_cols, cotangent):
    adj = adj_values.reshape(16, T, T)
    rows = tile_rows.reshape(16)
    cols = tile_cols.reshape(16)
    x_place = lax.axis_index("row") // 8
    y_place = lax.axis_index("col") // 4

    own = gather(gather(features, "zl"), "x").reshape(16, T, F)
    other = swap_core(own)
    partial, mine = call(
        forward_tiles,
        [((4, 4, T, F), BF), ((4, T, F), F32)],
        "ssvvv",
        [pltpu.VMEM((16, T, F), F32)],
    )(rows, cols, adj, own, other)
    parts = exchange(partial, "y")
    summed = add_received(mine, parts, y_place).astype(BF)
    parts = gather(jnp.concatenate([summed, cotangent[None]], axis=0), "zh")
    act, back = call(
        layer,
        [((T, F), F32), ((4, 6, T, F), BF)],
        "vvv",
        [pltpu.VMEM((4, T, F), F32)],
    )(parts[:, :4], parts[:, 4], weight)
    parts = exchange(back, "y")
    keep, send = call(
        backward_tiles,
        [((17, T, F), F32), ((17, T, F), F32)],
        "ssvv",
        [pltpu.VMEM((2, 16, T, F), F32)],
    )(rows, cols, adj, parts)
    total = keep + swap_core(send)
    tiles = total[:16].reshape(4, 4, T, F)
    high, low = split(total[16])
    parts = exchange(
        jnp.concatenate([tiles.astype(BF), spread(jnp.stack([high, low]))], axis=1), "x"
    )
    mine = lax.dynamic_index_in_dim(tiles, x_place, 0, keepdims=False)
    tiles = add_received(mine, parts[:, :4], x_place).astype(BF)
    high, low = split(jnp.sum(parts[:, 4:].astype(F32), axis=(0, 1)))
    parts = exchange(
        jnp.concatenate([tiles[:, None], spread(jnp.stack([high, low]))], axis=1), "zl"
    )
    parts = parts.astype(F32)
    out = jnp.sum(parts[:, 0], axis=0)
    grad = jnp.sum(parts[:, 1:], axis=(0, 1))
    return act, out, grad


def solution(mesh):
    return jax.shard_map(
        per_device,
        mesh=mesh,
        in_specs=(
            P(BOTH, None),
            P(),
            P("row", "col", None, None, None),
            P("row", "col", None),
            P("row", "col", None),
            P(BOTH, None),
        ),
        out_specs=(P(BOTH, None), P(BOTH, None), P()),
        check_vma=False,
    )
```

```python
import itertools

import jax
import jax.numpy as jnp
from jax import lax
from jax.experimental import pallas as pl
from jax.experimental.pallas import tpu as pltpu
from jax.sharding import PartitionSpec as P

BOTH = ("row", "col")
SIZES = {"x": 4, "zl": 4, "core": 2, "y": 4, "zh": 4}
F = 128
T = 128
BF = jnp.bfloat16
F32 = jnp.float32


def position(place):
    n = 0
    for name, size in SIZES.items():
        n = n * size + place[name]
    return n


def places():
    for values in itertools.product(*(range(s) for s in SIZES.values())):
        yield dict(zip(SIZES, values))


def groups(axis):
    found = {}
    for place in places():
        key = tuple(v for n, v in place.items() if n != axis)
        found.setdefault(key, []).append(position(place))
    return list(found.values())


def swap_core(array):
    pairs = [(position(p), position({**p, "core": 1 - p["core"]})) for p in places()]
    return lax.ppermute(array, BOTH, pairs)


def gather(array, axis):
    return lax.all_gather(array, BOTH, axis=0, tiled=False, axis_index_groups=groups(axis))


def exchange(array, axis):
    return lax.all_to_all(array, BOTH, 0, 0, tiled=True, axis_index_groups=groups(axis))


def spread(array):
    return jnp.broadcast_to(array[None], (4, *array.shape))


def core_place():
    return lax.rem(lax.axis_index("row"), 2)


def zl_place():
    return lax.rem(lax.div(lax.axis_index("row"), 2), 4)


def x_place():
    return lax.div(lax.axis_index("row"), 8)


def zh_place():
    return lax.rem(lax.axis_index("col"), 4)


def y_place():
    return lax.div(lax.axis_index("col"), 4)


def dot(a, b, dims):
    return lax.dot_general(a, b, (dims, ((), ())), preferred_element_type=F32)


def call(body, outs, spaces, scratch=()):
    kinds = {"v": pltpu.VMEM, "s": pltpu.SMEM}
    return pl.pallas_call(
        body,
        out_shape=[jax.ShapeDtypeStruct(s, d) for s, d in outs],
        in_specs=[pl.BlockSpec(memory_space=kinds[k]) for k in spaces],
        out_specs=[pl.BlockSpec(memory_space=pltpu.VMEM) for _ in outs],
        scratch_shapes=list(scratch),
        compiler_params=pltpu.CompilerParams(vmem_limit_bytes=16 << 20),
    )


def split(grad):
    high = grad.astype(BF)
    return high, (grad - high.astype(F32)).astype(BF)


def plus_others(own, parts, place, count):
    for j in range(1, 4):
        own += parts[lax.rem(place + j, 4), pl.ds(0, count)].astype(F32)
    return own


def forward_tiles(rows, cols, adj, own, other, out, mine, acc):
    acc[...] = jnp.zeros_like(acc)
    for t in range(16):
        b = cols[t]
        spot = lax.div(b, 2)
        x = jnp.where(lax.rem(b, 2) == core_place(), own[spot], other[spot])
        r = rows[t]
        acc[r] += dot(adj[t], x, ((1,), (0,)))
    out[...] = acc[...].astype(BF).reshape(4, 4, T, F)
    mine[...] = acc[pl.ds(y_place() * 4, 4)]


def add_y(parts, mine, cot, out):
    out[pl.ds(0, 4)] = plus_others(mine[...], parts, y_place(), 4).astype(BF)
    out[4] = cot[...]


def layer(parts, weight, act, out, kept):
    total = parts[0, pl.ds(0, 4)].astype(F32)
    for k in range(1, 4):
        total += parts[k, pl.ds(0, 4)].astype(F32)
    zed = total.reshape(512, F).astype(BF)
    w = weight[...]
    pre = dot(zed, w, ((1,), (0,)))
    sig = jax.nn.sigmoid(pre)
    kept[...] = (pre * sig).reshape(4, T, F)
    act[...] = kept[zh_place()]
    cot = jnp.concatenate([parts[k, 4] for k in range(4)], axis=0)
    dpre = (cot.astype(F32) * sig * (1.0 + pre * (1.0 - sig))).astype(BF)
    back = dot(dpre, w, ((1,), (1,))).astype(BF).reshape(4, T, F)
    grad = dot(zed, dpre, ((0,), (0,))).astype(BF)
    for k in range(4):
        out[k, pl.ds(0, 4)] = back
        out[k, 4] = grad


def backward_tiles(rows, cols, adj, parts, keep, send, acc, total):
    core = core_place()
    acc[...] = jnp.zeros_like(acc)
    for t in range(16):
        r = rows[t]
        b = cols[t]
        d = parts[lax.div(r, 4), lax.rem(r, 4)]
        acc[lax.rem(b, 2), lax.div(b, 2)] += dot(adj[t], d, ((0,), (0,)))
    grad = parts[0, 4].astype(F32)
    for k in range(1, 4):
        grad += parts[k, 4].astype(F32)
    total[...] = grad.reshape(2, 64, F)
    for ref, c in ((keep, core), (send, 1 - core)):
        ref[pl.ds(0, 2048), :] = acc[c].reshape(2048, F)
        ref[pl.ds(2048, 64), :] = total[c]


def add_cores(keep, got, out, mine):
    total = (keep[pl.ds(0, 2048), :] + got[pl.ds(0, 2048), :]).reshape(4, 4, T, F)
    high, low = split(keep[pl.ds(2048, 64), :] + got[pl.ds(2048, 64), :])
    for k in range(4):
        out[k, pl.ds(0, 4)] = total[k].astype(BF)
        out[k, 4, pl.ds(0, 64), :] = high
        out[k, 4, pl.ds(64, 64), :] = low
    start = pl.multiple_of(x_place() * 512, 512)
    own = keep[pl.ds(start, 512), :] + got[pl.ds(start, 512), :]
    mine[...] = own.reshape(4, T, F)


def sum_halves(parts, spot):
    total = parts[0, spot].astype(F32)
    for k in range(1, 4):
        total += parts[k, spot].astype(F32)
    return total[:64] + total[64:]


def add_x(parts, mine, out, own, kept):
    total = plus_others(mine[...], parts, x_place(), 4)
    high, low = split(sum_halves(parts, 4))
    for k in range(4):
        out[k, 0] = total[k].astype(BF)
        out[k, 1, pl.ds(0, 64), :] = high
        out[k, 1, pl.ds(64, 64), :] = low
    kept[...] = total
    own[...] = kept[zl_place()]


def add_z(parts, own, out, half):
    total = own[...]
    for j in range(1, 4):
        total += parts[lax.rem(zl_place() + j, 4), 0].astype(F32)
    out[...] = total
    half[...] = sum_halves(parts, 1)


def join(half, got, grad):
    core = core_place()
    grad[core] = half[...]
    grad[1 - core] = got[...]


def per_device(features, weight, adj_values, tile_rows, tile_cols, cotangent):
    adj = adj_values.reshape(16, T, T)
    rows = tile_rows.reshape(16)
    cols = tile_cols.reshape(16)
    tile = (T, F)

    own = exchange(spread(exchange(spread(features), "zl")), "x").reshape(16, T, F)
    other = swap_core(own)
    partial, mine = call(
        forward_tiles,
        [((4, 4, T, F), BF), ((4, T, F), F32)],
        "ssvvv",
        [pltpu.VMEM((16, T, F), F32)],
    )(rows, cols, adj, own, other)
    parts = exchange(partial, "y")
    (summed,) = call(add_y, [((5, T, F), BF)], "vvv")(parts, mine, cotangent)
    parts = gather(summed, "zh")
    act, back = call(
        layer, [(tile, F32), ((4, 5, T, F), BF)], "vv", [pltpu.VMEM((4, T, F), F32)]
    )(parts, weight)
    parts = exchange(back, "y")
    keep, send = call(
        backward_tiles,
        [((2112, F), F32), ((2112, F), F32)],
        "ssvv",
        [pltpu.VMEM((2, 16, T, F), F32), pltpu.VMEM((2, 64, F), F32)],
    )(rows, cols, adj, parts)
    got = swap_core(send)
    parts, mine = call(add_cores, [((4, 5, T, F), BF), ((4, T, F), F32)], "vv")(keep, got)
    parts = exchange(parts, "x")
    parts, own = call(
        add_x, [((4, 2, T, F), BF), (tile, F32)], "vv", [pltpu.VMEM((4, T, F), F32)]
    )(parts, mine)
    parts = exchange(parts, "zl")
    out, half = call(add_z, [(tile, F32), ((64, F), F32)], "vv")(parts, own)
    (grad,) = call(join, [((2, 64, F), F32)], "vv")(half, swap_core(half))
    return act, out, grad.reshape(F, F)


def solution(mesh):
    return jax.shard_map(
        per_device,
        mesh=mesh,
        in_specs=(
            P(BOTH, None),
            P(),
            P("row", "col", None, None, None),
            P("row", "col", None),
            P("row", "col", None),
            P(BOTH, None),
        ),
        out_specs=(P(BOTH, None), P(BOTH, None), P()),
        check_vma=False,
    )
```

```python
import itertools

import jax
import jax.numpy as jnp
from jax import lax
from jax.experimental import pallas as pl
from jax.experimental.pallas import tpu as pltpu
from jax.sharding import PartitionSpec as P

BOTH = ("row", "col")
SIZES = {"x": 4, "zl": 4, "core": 2, "y": 4, "zh": 4}
F = 128
T = 128
BF = jnp.bfloat16
F32 = jnp.float32


def position(place):
    n = 0
    for name, size in SIZES.items():
        n = n * size + place[name]
    return n


def places():
    for values in itertools.product(*(range(s) for s in SIZES.values())):
        yield dict(zip(SIZES, values))


def groups(axis):
    found = {}
    for place in places():
        key = tuple(v for n, v in place.items() if n != axis)
        found.setdefault(key, []).append(position(place))
    return list(found.values())


def swap_core(array):
    pairs = [(position(p), position({**p, "core": 1 - p["core"]})) for p in places()]
    return lax.ppermute(array, BOTH, pairs)


def gather(array, axis):
    return lax.all_gather(array, BOTH, axis=0, tiled=False, axis_index_groups=groups(axis))


def exchange(array, axis):
    return lax.all_to_all(array, BOTH, 0, 0, tiled=True, axis_index_groups=groups(axis))


def spread(array):
    return jnp.broadcast_to(array[None], (4, *array.shape))


def core_place():
    return lax.rem(lax.axis_index("row"), 2)


def zl_place():
    return lax.rem(lax.div(lax.axis_index("row"), 2), 4)


def x_place():
    return lax.div(lax.axis_index("row"), 8)


def zh_place():
    return lax.rem(lax.axis_index("col"), 4)


def y_place():
    return lax.div(lax.axis_index("col"), 4)


def dot(a, b, dims):
    return lax.dot_general(a, b, (dims, ((), ())), preferred_element_type=F32)


def call(body, outs, spaces, scratch=()):
    kinds = {"v": pltpu.VMEM, "s": pltpu.SMEM}
    return pl.pallas_call(
        body,
        out_shape=[jax.ShapeDtypeStruct(s, d) for s, d in outs],
        in_specs=[pl.BlockSpec(memory_space=kinds[k]) for k in spaces],
        out_specs=[pl.BlockSpec(memory_space=pltpu.VMEM) for _ in outs],
        scratch_shapes=list(scratch),
        compiler_params=pltpu.CompilerParams(vmem_limit_bytes=16 << 20),
    )


def split(grad):
    high = grad.astype(BF)
    return high, (grad - high.astype(F32)).astype(BF)


def plus_others(own, parts, place, count):
    for j in range(1, 4):
        own += parts[lax.rem(place + j, 4), pl.ds(0, count)].astype(F32)
    return own


def forward_tiles(rows, cols, adj, own, other, out, mine, acc):
    acc[...] = jnp.zeros_like(acc)
    for t in range(16):
        b = cols[t]
        spot = lax.div(b, 2)
        x = jnp.where(lax.rem(b, 2) == core_place(), own[spot], other[spot])
        r = rows[t]
        acc[r] += dot(adj[t], x, ((1,), (0,)))
    out[...] = acc[...].astype(BF).reshape(4, 4, T, F)
    mine[...] = acc[pl.ds(y_place() * 4, 4)]


def add_y(parts, mine, cot, out):
    out[pl.ds(0, 4)] = plus_others(mine[...], parts, y_place(), 4).astype(BF)
    out[4] = cot[...]


def layer(parts, weight, act, out, kept):
    total = parts[0, pl.ds(0, 4)].astype(F32)
    for k in range(1, 4):
        total += parts[k, pl.ds(0, 4)].astype(F32)
    zed = total.reshape(512, F).astype(BF)
    w = weight[...]
    pre = dot(zed, w, ((1,), (0,)))
    sig = jax.nn.sigmoid(pre)
    kept[...] = (pre * sig).reshape(4, T, F)
    act[...] = kept[zh_place()]
    cot = jnp.concatenate([parts[k, 4] for k in range(4)], axis=0)
    dpre = (cot.astype(F32) * sig * (1.0 + pre * (1.0 - sig))).astype(BF)
    back = dot(dpre, w, ((1,), (1,))).astype(BF).reshape(4, T, F)
    grad = dot(zed, dpre, ((0,), (0,))).astype(BF)
    for k in range(4):
        out[k, pl.ds(0, 4)] = back
        out[k, 4] = grad


def backward_tiles(rows, cols, adj, parts, keep, send, acc):
    core = core_place()
    acc[...] = jnp.zeros_like(acc)
    for t in range(16):
        r = rows[t]
        b = cols[t]
        d = parts[lax.div(r, 4), lax.rem(r, 4)]
        acc[lax.rem(b, 2), lax.div(b, 2)] += dot(adj[t], d, ((0,), (0,)))
    grad = parts[0, 4].astype(F32)
    for k in range(1, 4):
        grad += parts[k, 4].astype(F32)
    high, low = split(grad)
    keep[pl.ds(0, 16)] = acc[core]
    send[pl.ds(0, 16)] = acc[1 - core].astype(BF)
    keep[16] = high.astype(F32) + low.astype(F32)
    send[16] = high
    send[17] = low


def add_cores(keep, got, out, mine):
    high, low = split(keep[16] + (got[16].astype(F32) + got[17].astype(F32)))
    for k in range(4):
        total = keep[pl.ds(4 * k, 4)] + got[pl.ds(4 * k, 4)].astype(F32)
        out[k, pl.ds(0, 4)] = total.astype(BF)
        out[k, 4] = high
        out[k, 5] = low
    start = x_place() * 4
    mine[...] = keep[pl.ds(start, 4)] + got[pl.ds(start, 4)].astype(F32)


def sum_grad(parts, spot):
    total = parts[0, spot].astype(F32) + parts[0, spot + 1].astype(F32)
    for k in range(1, 4):
        total += parts[k, spot].astype(F32) + parts[k, spot + 1].astype(F32)
    return total


def add_x(parts, mine, out, own, kept):
    total = plus_others(mine[...], parts, x_place(), 4)
    high, low = split(sum_grad(parts, 4))
    for k in range(4):
        out[k, 0] = total[k].astype(BF)
        out[k, 1] = high
        out[k, 2] = low
    kept[...] = total
    own[...] = kept[zl_place()]


def add_z(parts, own, out, grad):
    total = own[...]
    for j in range(1, 4):
        total += parts[lax.rem(zl_place() + j, 4), 0].astype(F32)
    out[...] = total
    grad[...] = sum_grad(parts, 1)


def per_device(features, weight, adj_values, tile_rows, tile_cols, cotangent):
    adj = adj_values.reshape(16, T, T)
    rows = tile_rows.reshape(16)
    cols = tile_cols.reshape(16)
    tile = (T, F)

    own = exchange(spread(exchange(spread(features), "zl")), "x").reshape(16, T, F)
    other = swap_core(own)
    partial, mine = call(
        forward_tiles,
        [((4, 4, T, F), BF), ((4, T, F), F32)],
        "ssvvv",
        [pltpu.VMEM((16, T, F), F32)],
    )(rows, cols, adj, own, other)
    parts = exchange(partial, "y")
    (summed,) = call(add_y, [((5, T, F), BF)], "vvv")(parts, mine, cotangent)
    parts = gather(summed, "zh")
    act, back = call(
        layer, [(tile, F32), ((4, 5, T, F), BF)], "vv", [pltpu.VMEM((4, T, F), F32)]
    )(parts, weight)
    parts = exchange(back, "y")
    keep, send = call(
        backward_tiles,
        [((17, T, F), F32), ((18, T, F), BF)],
        "ssvv",
        [pltpu.VMEM((2, 16, T, F), F32)],
    )(rows, cols, adj, parts)
    got = swap_core(send)
    parts, mine = call(add_cores, [((4, 6, T, F), BF), ((4, T, F), F32)], "vv")(keep, got)
    parts = exchange(parts, "x")
    parts, own = call(
        add_x, [((4, 3, T, F), BF), (tile, F32)], "vv", [pltpu.VMEM((4, T, F), F32)]
    )(parts, mine)
    parts = exchange(parts, "zl")
    out, grad = call(add_z, [(tile, F32), (tile, F32)], "vv")(parts, own)
    return act, out, grad


def solution(mesh):
    return jax.shard_map(
        per_device,
        mesh=mesh,
        in_specs=(
            P(BOTH, None),
            P(),
            P("row", "col", None, None, None),
            P("row", "col", None),
            P("row", "col", None),
            P(BOTH, None),
        ),
        out_specs=(P(BOTH, None), P(BOTH, None), P()),
        check_vma=False,
    )
```

```python
import itertools

import jax
import jax.numpy as jnp
from jax import lax
from jax.experimental import pallas as pl
from jax.experimental.pallas import tpu as pltpu
from jax.sharding import PartitionSpec as P

BOTH = ("row", "col")
SIZES = {"x": 4, "zl": 4, "core": 2, "y": 4, "zh": 4}
F = 128
T = 128
BF = jnp.bfloat16
F32 = jnp.float32


def position(place):
    n = 0
    for name, size in SIZES.items():
        n = n * size + place[name]
    return n


def places():
    for values in itertools.product(*(range(s) for s in SIZES.values())):
        yield dict(zip(SIZES, values))


def groups(*axes):
    found = {}
    for place in places():
        key = tuple(v for n, v in place.items() if n not in axes)
        found.setdefault(key, []).append(position(place))
    return list(found.values())


def swap_core(array):
    pairs = [(position(p), position({**p, "core": 1 - p["core"]})) for p in places()]
    return lax.ppermute(array, BOTH, pairs)


def gather(array, axis):
    return lax.all_gather(array, BOTH, axis=0, tiled=False, axis_index_groups=groups(axis))


def exchange(array, *axes):
    return lax.all_to_all(array, BOTH, 0, 0, tiled=True, axis_index_groups=groups(*axes))


def core_place():
    return lax.rem(lax.axis_index("row"), 2)


def zl_place():
    return lax.rem(lax.div(lax.axis_index("row"), 2), 4)


def x_place():
    return lax.div(lax.axis_index("row"), 8)


def zh_place():
    return lax.rem(lax.axis_index("col"), 4)


def y_place():
    return lax.div(lax.axis_index("col"), 4)


def dot(a, b, dims):
    return lax.dot_general(a, b, (dims, ((), ())), preferred_element_type=F32)


def call(body, outs, spaces, scratch=()):
    kinds = {"v": pltpu.VMEM, "s": pltpu.SMEM}
    return pl.pallas_call(
        body,
        out_shape=[jax.ShapeDtypeStruct(s, d) for s, d in outs],
        in_specs=[pl.BlockSpec(memory_space=kinds[k]) for k in spaces],
        out_specs=[pl.BlockSpec(memory_space=pltpu.VMEM) for _ in outs],
        scratch_shapes=list(scratch),
        compiler_params=pltpu.CompilerParams(vmem_limit_bytes=16 << 20),
    )


def split(grad):
    high = grad.astype(BF)
    return high, (grad - high.astype(F32)).astype(BF)


def plus_others(own, parts, place, count):
    for j in range(1, 4):
        own += parts[lax.rem(place + j, 4), pl.ds(0, count)].astype(F32)
    return own


def forward_tiles(rows, cols, adj, own, other, out, mine, acc):
    acc[...] = jnp.zeros_like(acc)
    for t in range(16):
        b = cols[t]
        spot = lax.div(b, 2)
        x = jnp.where(lax.rem(b, 2) == core_place(), own[spot], other[spot])
        r = rows[t]
        acc[r] += dot(adj[t], x, ((1,), (0,)))
    out[...] = acc[...].astype(BF).reshape(4, 4, T, F)
    mine[...] = acc[pl.ds(y_place() * 4, 4)]


def add_y(parts, mine, cot, out):
    out[pl.ds(0, 4)] = plus_others(mine[...], parts, y_place(), 4).astype(BF)
    out[4] = cot[...]


def layer(parts, weight, act, out, kept):
    total = parts[0, pl.ds(0, 4)].astype(F32)
    for k in range(1, 4):
        total += parts[k, pl.ds(0, 4)].astype(F32)
    zed = total.reshape(512, F).astype(BF)
    w = weight[...]
    pre = dot(zed, w, ((1,), (0,)))
    sig = jax.nn.sigmoid(pre)
    kept[...] = (pre * sig).reshape(4, T, F)
    act[...] = kept[zh_place()]
    cot = jnp.concatenate([parts[k, 4] for k in range(4)], axis=0)
    dpre = (cot.astype(F32) * sig * (1.0 + pre * (1.0 - sig))).astype(BF)
    back = dot(dpre, w, ((1,), (1,))).astype(BF).reshape(4, T, F)
    high, low = split(dot(zed, dpre, ((0,), (0,))))
    for k in range(4):
        out[k, pl.ds(0, 4)] = back
        out[k, 4] = high
        out[k, 5] = low


def backward_tiles(rows, cols, adj, parts, keep, send, acc):
    core = core_place()
    acc[...] = jnp.zeros_like(acc)
    for t in range(16):
        r = rows[t]
        b = cols[t]
        d = parts[lax.div(r, 4), lax.rem(r, 4)]
        acc[lax.rem(b, 2), lax.div(b, 2)] += dot(adj[t], d, ((0,), (0,)))
    high, low = split(sum_grad(parts, 4))
    keep[pl.ds(0, 16)] = acc[core]
    send[pl.ds(0, 16)] = acc[1 - core].astype(BF)
    keep[16] = high.astype(F32) + low.astype(F32)
    send[16] = high
    send[17] = low


def add_cores(keep, got, out, mine):
    high, low = split(keep[16] + (got[16].astype(F32) + got[17].astype(F32)))
    for k in range(4):
        total = keep[pl.ds(4 * k, 4)] + got[pl.ds(4 * k, 4)].astype(F32)
        out[k, pl.ds(0, 4)] = total.astype(BF)
        out[k, 4] = high
        out[k, 5] = low
    start = x_place() * 4
    mine[...] = keep[pl.ds(start, 4)] + got[pl.ds(start, 4)].astype(F32)


def sum_grad(parts, spot):
    total = parts[0, spot].astype(F32) + parts[0, spot + 1].astype(F32)
    for k in range(1, 4):
        total += parts[k, spot].astype(F32) + parts[k, spot + 1].astype(F32)
    return total


def add_x(parts, mine, out, own, kept):
    total = plus_others(mine[...], parts, x_place(), 4)
    grad = sum_grad(parts, 4).astype(BF)
    for k in range(4):
        out[k, 0] = total[k].astype(BF)
        out[k, 1] = grad
    kept[...] = total
    own[...] = kept[zl_place()]


def add_z(parts, own, out, grad):
    total = own[...]
    for j in range(1, 4):
        total += parts[lax.rem(zl_place() + j, 4), 0].astype(F32)
    out[...] = total
    total = parts[0, 1].astype(F32)
    for k in range(1, 4):
        total += parts[k, 1].astype(F32)
    grad[...] = total


def per_device(features, weight, adj_values, tile_rows, tile_cols, cotangent):
    adj = adj_values.reshape(16, T, T)
    rows = tile_rows.reshape(16)
    cols = tile_cols.reshape(16)
    tile = (T, F)

    own = exchange(jnp.broadcast_to(features[None], (16, T, F)), "x", "zl")
    other = swap_core(own)
    partial, mine = call(
        forward_tiles,
        [((4, 4, T, F), BF), ((4, T, F), F32)],
        "ssvvv",
        [pltpu.VMEM((16, T, F), F32)],
    )(rows, cols, adj, own, other)
    parts = exchange(partial, "y")
    (summed,) = call(add_y, [((5, T, F), BF)], "vvv")(parts, mine, cotangent)
    parts = gather(summed, "zh")
    act, back = call(
        layer, [(tile, F32), ((4, 6, T, F), BF)], "vv", [pltpu.VMEM((4, T, F), F32)]
    )(parts, weight)
    parts = exchange(back, "y")
    keep, send = call(
        backward_tiles,
        [((17, T, F), F32), ((18, T, F), BF)],
        "ssvv",
        [pltpu.VMEM((2, 16, T, F), F32)],
    )(rows, cols, adj, parts)
    got = swap_core(send)
    parts, mine = call(add_cores, [((4, 6, T, F), BF), ((4, T, F), F32)], "vv")(keep, got)
    parts = exchange(parts, "x")
    parts, own = call(
        add_x, [((4, 2, T, F), BF), (tile, F32)], "vv", [pltpu.VMEM((4, T, F), F32)]
    )(parts, mine)
    parts = exchange(parts, "zl")
    out, grad = call(add_z, [(tile, F32), (tile, F32)], "vv")(parts, own)
    return act, out, grad


def solution(mesh):
    return jax.shard_map(
        per_device,
        mesh=mesh,
        in_specs=(
            P(BOTH, None),
            P(),
            P("row", "col", None, None, None),
            P("row", "col", None),
            P("row", "col", None),
            P(BOTH, None),
        ),
        out_specs=(P(BOTH, None), P(BOTH, None), P()),
        check_vma=False,
    )
```

```python
import itertools

import jax
import jax.numpy as jnp
from jax import lax
from jax.experimental import pallas as pl
from jax.experimental.pallas import tpu as pltpu
from jax.sharding import PartitionSpec as P

BOTH = ("row", "col")
SIZES = {"x": 4, "zl": 4, "core": 2, "y": 4, "zh": 4}
F = 128
T = 128
BF = jnp.bfloat16
F32 = jnp.float32


def position(place):
    n = 0
    for name, size in SIZES.items():
        n = n * size + place[name]
    return n


def places():
    for values in itertools.product(*(range(s) for s in SIZES.values())):
        yield dict(zip(SIZES, values))


def groups(*axes):
    found = {}
    for place in places():
        key = tuple(v for n, v in place.items() if n not in axes)
        found.setdefault(key, []).append(position(place))
    return list(found.values())


def swap_core(array):
    pairs = [(position(p), position({**p, "core": 1 - p["core"]})) for p in places()]
    return lax.ppermute(array, BOTH, pairs)


def gather(array, axis):
    return lax.all_gather(array, BOTH, axis=0, tiled=False, axis_index_groups=groups(axis))


def exchange(array, *axes):
    return lax.all_to_all(array, BOTH, 0, 0, tiled=True, axis_index_groups=groups(*axes))


def core_place():
    return lax.rem(lax.axis_index("row"), 2)


def zl_place():
    return lax.rem(lax.div(lax.axis_index("row"), 2), 4)


def x_place():
    return lax.div(lax.axis_index("row"), 8)


def zh_place():
    return lax.rem(lax.axis_index("col"), 4)


def y_place():
    return lax.div(lax.axis_index("col"), 4)


def dot(a, b, dims):
    return lax.dot_general(a, b, (dims, ((), ())), preferred_element_type=F32)


def call(body, outs, spaces, scratch=()):
    kinds = {"v": pltpu.VMEM, "s": pltpu.SMEM}
    return pl.pallas_call(
        body,
        out_shape=[jax.ShapeDtypeStruct(s, d) for s, d in outs],
        in_specs=[pl.BlockSpec(memory_space=kinds[k]) for k in spaces],
        out_specs=[pl.BlockSpec(memory_space=pltpu.VMEM) for _ in outs],
        scratch_shapes=list(scratch),
        compiler_params=pltpu.CompilerParams(vmem_limit_bytes=16 << 20),
    )


def split(grad):
    high = grad.astype(BF)
    return high, (grad - high.astype(F32)).astype(BF)


def plus_others(own, parts, place, count):
    for j in range(1, 4):
        own += parts[lax.rem(place + j, 4), pl.ds(0, count)].astype(F32)
    return own


def forward_tiles(rows, cols, adj, own, other, out, mine, acc):
    acc[...] = jnp.zeros_like(acc)
    for t in range(16):
        b = cols[t]
        spot = lax.div(b, 2)
        x = jnp.where(lax.rem(b, 2) == core_place(), own[spot], other[spot])
        r = rows[t]
        acc[r] += dot(adj[t], x, ((1,), (0,)))
    out[...] = acc[...].astype(BF).reshape(4, 4, T, F)
    mine[...] = acc[pl.ds(y_place() * 4, 4)]


def add_y(parts, mine, cot, out):
    out[pl.ds(0, 4)] = plus_others(mine[...], parts, y_place(), 4).astype(BF)
    out[4] = cot[...]


def layer(parts, weight, act, out, kept):
    total = parts[0, pl.ds(0, 4)].astype(F32)
    for k in range(1, 4):
        total += parts[k, pl.ds(0, 4)].astype(F32)
    zed, zed_low = split(total.reshape(512, F))
    w = weight[...]
    pre = dot(zed, w, ((1,), (0,))) + dot(zed_low, w, ((1,), (0,)))
    sig = jax.nn.sigmoid(pre)
    kept[...] = (pre * sig).reshape(4, T, F)
    act[...] = kept[zh_place()]
    cot = jnp.concatenate([parts[k, 4] for k in range(4)], axis=0)
    dpre, dpre_low = split(cot.astype(F32) * sig * (1.0 + pre * (1.0 - sig)))
    back = dot(dpre, w, ((1,), (1,))) + dot(dpre_low, w, ((1,), (1,)))
    back = back.astype(BF).reshape(4, T, F)
    rows = ((0,), (0,))
    grad = dot(zed, dpre, rows) + dot(zed_low, dpre, rows) + dot(zed, dpre_low, rows)
    high, low = split(grad)
    for k in range(4):
        out[k, pl.ds(0, 4)] = back
        out[k, 4] = high
        out[k, 5] = low


def backward_tiles(rows, cols, adj, parts, keep, send, acc):
    core = core_place()
    acc[...] = jnp.zeros_like(acc)
    for t in range(16):
        r = rows[t]
        b = cols[t]
        d = parts[lax.div(r, 4), lax.rem(r, 4)]
        acc[lax.rem(b, 2), lax.div(b, 2)] += dot(adj[t], d, ((0,), (0,)))
    high, low = split(sum_of(parts, 4) + sum_of(parts, 5))
    keep[pl.ds(0, 16)] = acc[core]
    send[pl.ds(0, 16)] = acc[1 - core].astype(BF)
    keep[16] = high.astype(F32) + low.astype(F32)
    send[16] = high
    send[17] = low


def add_cores(keep, got, out, mine):
    grad = (keep[16] + (got[16].astype(F32) + got[17].astype(F32))).astype(BF)
    for k in range(4):
        total = keep[pl.ds(4 * k, 4)] + got[pl.ds(4 * k, 4)].astype(F32)
        out[k, pl.ds(0, 4)] = total.astype(BF)
        out[k, 4] = grad
    start = x_place() * 4
    mine[...] = keep[pl.ds(start, 4)] + got[pl.ds(start, 4)].astype(F32)


def sum_of(parts, spot):
    total = parts[0, spot].astype(F32)
    for k in range(1, 4):
        total += parts[k, spot].astype(F32)
    return total


def add_x(parts, mine, out, own, kept):
    total = plus_others(mine[...], parts, x_place(), 4)
    grad = sum_of(parts, 4).astype(BF)
    for k in range(4):
        out[k, 0] = total[k].astype(BF)
        out[k, 1] = grad
    kept[...] = total
    own[...] = kept[zl_place()]


def add_z(parts, own, out, grad):
    total = own[...]
    for j in range(1, 4):
        total += parts[lax.rem(zl_place() + j, 4), 0].astype(F32)
    out[...] = total
    grad[...] = sum_of(parts, 1)


def per_device(features, weight, adj_values, tile_rows, tile_cols, cotangent):
    adj = adj_values.reshape(16, T, T)
    rows = tile_rows.reshape(16)
    cols = tile_cols.reshape(16)
    tile = (T, F)

    own = exchange(jnp.broadcast_to(features[None], (4, T, F)), "zl")
    own = exchange(jnp.broadcast_to(own[None], (4, 4, T, F)), "x").reshape(16, T, F)
    other = swap_core(own)
    partial, mine = call(
        forward_tiles,
        [((4, 4, T, F), BF), ((4, T, F), F32)],
        "ssvvv",
        [pltpu.VMEM((16, T, F), F32)],
    )(rows, cols, adj, own, other)
    parts = exchange(partial, "y")
    (summed,) = call(add_y, [((5, T, F), BF)], "vvv")(parts, mine, cotangent)
    parts = gather(summed, "zh")
    act, back = call(
        layer, [(tile, F32), ((4, 6, T, F), BF)], "vv", [pltpu.VMEM((4, T, F), F32)]
    )(parts, weight)
    parts = exchange(back, "y")
    keep, send = call(
        backward_tiles,
        [((17, T, F), F32), ((18, T, F), BF)],
        "ssvv",
        [pltpu.VMEM((2, 16, T, F), F32)],
    )(rows, cols, adj, parts)
    got = swap_core(send)
    parts, mine = call(add_cores, [((4, 5, T, F), BF), ((4, T, F), F32)], "vv")(keep, got)
    parts = exchange(parts, "x")
    parts, own = call(
        add_x, [((4, 2, T, F), BF), (tile, F32)], "vv", [pltpu.VMEM((4, T, F), F32)]
    )(parts, mine)
    parts = exchange(parts, "zl")
    out, grad = call(add_z, [(tile, F32), (tile, F32)], "vv")(parts, own)
    return act, out, grad


def solution(mesh):
    return jax.shard_map(
        per_device,
        mesh=mesh,
        in_specs=(
            P(BOTH, None),
            P(),
            P("row", "col", None, None, None),
            P("row", "col", None),
            P("row", "col", None),
            P(BOTH, None),
        ),
        out_specs=(P(BOTH, None), P(BOTH, None), P()),
        check_vma=False,
    )
```

```python
import itertools

import jax
import jax.numpy as jnp
from jax import lax
from jax.experimental import pallas as pl
from jax.experimental.pallas import tpu as pltpu
from jax.sharding import PartitionSpec as P

BOTH = ("row", "col")
SIZES = {"x": 4, "zl": 4, "core": 2, "y": 4, "zh": 4}
F = 128
T = 128
BF = jnp.bfloat16
F32 = jnp.float32


def position(place):
    n = 0
    for name, size in SIZES.items():
        n = n * size + place[name]
    return n


def places():
    for values in itertools.product(*(range(s) for s in SIZES.values())):
        yield dict(zip(SIZES, values))


def groups(*axes):
    found = {}
    for place in places():
        key = tuple(v for n, v in place.items() if n not in axes)
        found.setdefault(key, []).append(position(place))
    return list(found.values())


def swap_core(array):
    pairs = [(position(p), position({**p, "core": 1 - p["core"]})) for p in places()]
    return lax.ppermute(array, BOTH, pairs)


def gather(array, axis):
    return lax.all_gather(array, BOTH, axis=0, tiled=False, axis_index_groups=groups(axis))


def exchange(array, *axes):
    return lax.all_to_all(array, BOTH, 0, 0, tiled=True, axis_index_groups=groups(*axes))


def core_place():
    return lax.rem(lax.axis_index("row"), 2)


def zl_place():
    return lax.rem(lax.div(lax.axis_index("row"), 2), 4)


def x_place():
    return lax.div(lax.axis_index("row"), 8)


def zh_place():
    return lax.rem(lax.axis_index("col"), 4)


def y_place():
    return lax.div(lax.axis_index("col"), 4)


def dot(a, b, dims):
    return lax.dot_general(a, b, (dims, ((), ())), preferred_element_type=F32)


def copies(source, out):
    for k in range(4):
        out[k] = source[...]


def call(body, outs, spaces, scratch=()):
    kinds = {"v": pltpu.VMEM, "s": pltpu.SMEM}
    return pl.pallas_call(
        body,
        out_shape=[jax.ShapeDtypeStruct(s, d) for s, d in outs],
        in_specs=[pl.BlockSpec(memory_space=kinds[k]) for k in spaces],
        out_specs=[pl.BlockSpec(memory_space=pltpu.VMEM) for _ in outs],
        scratch_shapes=list(scratch),
        compiler_params=pltpu.CompilerParams(vmem_limit_bytes=16 << 20),
    )


def split(grad):
    high = grad.astype(BF)
    return high, (grad - high.astype(F32)).astype(BF)


def plus_others(own, parts, place, count):
    for j in range(1, 4):
        own += parts[lax.rem(place + j, 4), pl.ds(0, count)].astype(F32)
    return own


def forward_tiles(rows, cols, adj, own, other, out, mine, acc):
    acc[...] = jnp.zeros_like(acc)
    for t in range(16):
        b = cols[t]
        spot = lax.div(b, 2)
        x = jnp.where(lax.rem(b, 2) == core_place(), own[spot], other[spot])
        r = rows[t]
        acc[r] += dot(adj[t], x, ((1,), (0,)))
    out[...] = acc[...].astype(BF).reshape(4, 4, T, F)
    mine[...] = acc[pl.ds(y_place() * 4, 4)]


def add_y(parts, mine, cot, out):
    out[pl.ds(0, 4)] = plus_others(mine[...], parts, y_place(), 4).astype(BF)
    out[4] = cot[...]


def layer(parts, weight, act, out, kept):
    total = parts[0, pl.ds(0, 4)].astype(F32)
    for k in range(1, 4):
        total += parts[k, pl.ds(0, 4)].astype(F32)
    zed, zed_low = split(total.reshape(512, F))
    w = weight[...]
    pre = dot(zed, w, ((1,), (0,))) + dot(zed_low, w, ((1,), (0,)))
    sig = jax.nn.sigmoid(pre)
    kept[...] = (pre * sig).reshape(4, T, F)
    act[...] = kept[zh_place()]
    cot = jnp.concatenate([parts[k, 4] for k in range(4)], axis=0)
    dpre, dpre_low = split(cot.astype(F32) * sig * (1.0 + pre * (1.0 - sig)))
    back = dot(dpre, w, ((1,), (1,))) + dot(dpre_low, w, ((1,), (1,)))
    back = back.astype(BF).reshape(4, T, F)
    rows = ((0,), (0,))
    grad = dot(zed, dpre, rows) + dot(zed_low, dpre, rows) + dot(zed, dpre_low, rows)
    high, low = split(grad)
    for k in range(4):
        out[k, pl.ds(0, 4)] = back
        out[k, 4] = high
        out[k, 5] = low


def backward_tiles(rows, cols, adj, parts, acc, grad, send):
    core = core_place()
    acc[...] = jnp.zeros_like(acc)
    for t in range(16):
        r = rows[t]
        b = cols[t]
        d = parts[lax.div(r, 4), lax.rem(r, 4)]
        acc[lax.rem(b, 2), lax.div(b, 2)] += dot(adj[t], d, ((0,), (0,)))
    high, low = split(sum_of(parts, 4) + sum_of(parts, 5))
    send[pl.ds(0, 16)] = acc[1 - core].astype(BF)
    grad[...] = high.astype(F32) + low.astype(F32)
    send[16] = high
    send[17] = low


def add_cores(keeps, kept_grad, got, out, mine):
    keep = keeps.at[core_place()]
    grad = (kept_grad[...] + (got[16].astype(F32) + got[17].astype(F32))).astype(BF)
    for k in range(4):
        total = keep[pl.ds(4 * k, 4)] + got[pl.ds(4 * k, 4)].astype(F32)
        out[k, pl.ds(0, 4)] = total.astype(BF)
        out[k, 4] = grad
    start = x_place() * 4
    mine[...] = keep[pl.ds(start, 4)] + got[pl.ds(start, 4)].astype(F32)


def sum_of(parts, spot):
    total = parts[0, spot].astype(F32)
    for k in range(1, 4):
        total += parts[k, spot].astype(F32)
    return total


def add_x(parts, mine, out, own, kept):
    total = plus_others(mine[...], parts, x_place(), 4)
    grad = sum_of(parts, 4).astype(BF)
    for k in range(4):
        out[k, 0] = total[k].astype(BF)
        out[k, 1] = grad
    kept[...] = total
    own[...] = kept[zl_place()]


def add_z(parts, own, layer_act, out, grad, act):
    act[...] = layer_act[...]
    total = own[...]
    for j in range(1, 4):
        total += parts[lax.rem(zl_place() + j, 4), 0].astype(F32)
    out[...] = total
    grad[...] = sum_of(parts, 1)


def per_device(features, weight, adj_values, tile_rows, tile_cols, cotangent):
    adj = adj_values.reshape(16, T, T)
    rows = tile_rows.reshape(16)
    cols = tile_cols.reshape(16)
    tile = (T, F)

    (own,) = call(copies, [((4, T, F), BF)], "v")(features)
    own = exchange(own, "zl")
    own = exchange(jnp.broadcast_to(own[None], (4, 4, T, F)), "x").reshape(16, T, F)
    other = swap_core(own)
    partial, mine = call(
        forward_tiles,
        [((4, 4, T, F), BF), ((4, T, F), F32)],
        "ssvvv",
        [pltpu.VMEM((16, T, F), F32)],
    )(rows, cols, adj, own, other)
    parts = exchange(partial, "y")
    (summed,) = call(add_y, [((5, T, F), BF)], "vvv")(parts, mine, cotangent)
    parts = gather(summed, "zh")
    act, back = call(
        layer, [(tile, F32), ((4, 6, T, F), BF)], "vv", [pltpu.VMEM((4, T, F), F32)]
    )(parts, weight)
    parts = exchange(back, "y")
    keeps, grad, send = call(
        backward_tiles, [((2, 16, T, F), F32), (tile, F32), ((18, T, F), BF)], "ssvv"
    )(rows, cols, adj, parts)
    got = swap_core(send)
    parts, mine = call(add_cores, [((4, 5, T, F), BF), ((4, T, F), F32)], "vvv")(keeps, grad, got)
    parts = exchange(parts, "x")
    parts, own = call(
        add_x, [((4, 2, T, F), BF), (tile, F32)], "vv", [pltpu.VMEM((4, T, F), F32)]
    )(parts, mine)
    parts = exchange(parts, "zl")
    out, grad, act = call(add_z, [(tile, F32)] * 3, "vvv")(parts, own, act)
    return act, out, grad


def solution(mesh):
    return jax.shard_map(
        per_device,
        mesh=mesh,
        in_specs=(
            P(BOTH, None),
            P(),
            P("row", "col", None, None, None),
            P("row", "col", None),
            P("row", "col", None),
            P(BOTH, None),
        ),
        out_specs=(P(BOTH, None), P(BOTH, None), P()),
        check_vma=False,
    )
```

```python
import itertools

import jax
import jax.numpy as jnp
from jax import lax
from jax.experimental import pallas as pl
from jax.experimental.pallas import tpu as pltpu
from jax.sharding import PartitionSpec as P

BOTH = ("row", "col")
SIZES = {"x": 4, "zl": 4, "core": 2, "y": 4, "zh": 4}
F = 128
T = 128
BF = jnp.bfloat16
F32 = jnp.float32


def position(place):
    n = 0
    for name, size in SIZES.items():
        n = n * size + place[name]
    return n


def places():
    for values in itertools.product(*(range(s) for s in SIZES.values())):
        yield dict(zip(SIZES, values))


def groups(*axes):
    found = {}
    for place in places():
        key = tuple(v for n, v in place.items() if n not in axes)
        found.setdefault(key, []).append(position(place))
    return list(found.values())


def swap_core(array):
    pairs = [(position(p), position({**p, "core": 1 - p["core"]})) for p in places()]
    return lax.ppermute(array, BOTH, pairs)


def gather(array, axis):
    return lax.all_gather(array, BOTH, axis=0, tiled=False, axis_index_groups=groups(axis))


def exchange(array, *axes):
    return lax.all_to_all(array, BOTH, 0, 0, tiled=True, axis_index_groups=groups(*axes))


def core_place():
    return lax.rem(lax.axis_index("row"), 2)


def zl_place():
    return lax.rem(lax.div(lax.axis_index("row"), 2), 4)


def x_place():
    return lax.div(lax.axis_index("row"), 8)


def zh_place():
    return lax.rem(lax.axis_index("col"), 4)


def y_place():
    return lax.div(lax.axis_index("col"), 4)


def dot(a, b, dims):
    return lax.dot_general(a, b, (dims, ((), ())), preferred_element_type=F32)


def copies(source, out):
    for k in range(4):
        out[k] = source[...]


def call(body, outs, spaces, scratch=()):
    kinds = {"v": pltpu.VMEM, "s": pltpu.SMEM}
    return pl.pallas_call(
        body,
        out_shape=[jax.ShapeDtypeStruct(s, d) for s, d in outs],
        in_specs=[pl.BlockSpec(memory_space=kinds[k]) for k in spaces],
        out_specs=[pl.BlockSpec(memory_space=pltpu.VMEM) for _ in outs],
        scratch_shapes=list(scratch),
        compiler_params=pltpu.CompilerParams(vmem_limit_bytes=16 << 20),
    )


def split(grad):
    high = grad.astype(BF)
    return high, (grad - high.astype(F32)).astype(BF)


def plus_others(own, parts, place, count):
    for j in range(1, 4):
        own += parts[lax.rem(place + j, 4), pl.ds(0, count)].astype(F32)
    return own


def forward_tiles(rows, cols, adj, own, other, out, mine, acc, products):
    acc[...] = jnp.zeros_like(acc)
    for t in range(16):
        b = cols[t]
        spot = lax.div(b, 2)
        x = jnp.where(lax.rem(b, 2) == core_place(), own[spot], other[spot])
        products[t] = dot(adj[t], x, ((1,), (0,)))
    for t in range(16):
        acc[rows[t]] += products[t]
    out[...] = acc[...].astype(BF).reshape(4, 4, T, F)
    mine[...] = acc[pl.ds(y_place() * 4, 4)]


def add_y(parts, mine, cot, out):
    out[pl.ds(0, 4)] = plus_others(mine[...], parts, y_place(), 4).astype(BF)
    out[4] = cot[...]


def layer(parts, weight, act, out, kept):
    total = parts[0, pl.ds(0, 4)].astype(F32)
    for k in range(1, 4):
        total += parts[k, pl.ds(0, 4)].astype(F32)
    zed, zed_low = split(total.reshape(512, F))
    w = weight[...]
    pre = dot(zed, w, ((1,), (0,))) + dot(zed_low, w, ((1,), (0,)))
    sig = jax.nn.sigmoid(pre)
    kept[...] = (pre * sig).reshape(4, T, F)
    act[...] = kept[zh_place()]
    cot = jnp.concatenate([parts[k, 4] for k in range(4)], axis=0)
    dpre, dpre_low = split(cot.astype(F32) * sig * (1.0 + pre * (1.0 - sig)))
    back = dot(dpre, w, ((1,), (1,))) + dot(dpre_low, w, ((1,), (1,)))
    back = back.astype(BF).reshape(4, T, F)
    rows = ((0,), (0,))
    grad = dot(zed, dpre, rows) + dot(zed_low, dpre, rows) + dot(zed, dpre_low, rows)
    high, low = split(grad)
    for k in range(4):
        out[k, pl.ds(0, 4)] = back
        out[k, 4] = high
        out[k, 5] = low


def backward_tiles(rows, cols, adj, parts, acc, grad, send, products):
    core = core_place()
    acc[...] = jnp.zeros_like(acc)
    for t in range(16):
        r = rows[t]
        d = parts[lax.div(r, 4), lax.rem(r, 4)]
        products[t] = dot(adj[t], d, ((0,), (0,)))
    for t in range(16):
        b = cols[t]
        acc[lax.rem(b, 2), lax.div(b, 2)] += products[t]
    high, low = split(sum_of(parts, 4) + sum_of(parts, 5))
    send[pl.ds(0, 16)] = acc[1 - core].astype(BF)
    grad[...] = high.astype(F32) + low.astype(F32)
    send[16] = high
    send[17] = low


def add_cores(keeps, kept_grad, got, out, mine):
    keep = keeps.at[core_place()]
    grad = (kept_grad[...] + (got[16].astype(F32) + got[17].astype(F32))).astype(BF)
    for k in range(4):
        total = keep[pl.ds(4 * k, 4)] + got[pl.ds(4 * k, 4)].astype(F32)
        out[k, pl.ds(0, 4)] = total.astype(BF)
        out[k, 4] = grad
    start = x_place() * 4
    mine[...] = keep[pl.ds(start, 4)] + got[pl.ds(start, 4)].astype(F32)


def sum_of(parts, spot):
    total = parts[0, spot].astype(F32)
    for k in range(1, 4):
        total += parts[k, spot].astype(F32)
    return total


def add_x(parts, mine, out, own, kept):
    total = plus_others(mine[...], parts, x_place(), 4)
    grad = sum_of(parts, 4).astype(BF)
    for k in range(4):
        out[k, 0] = total[k].astype(BF)
        out[k, 1] = grad
    kept[...] = total
    own[...] = kept[zl_place()]


def add_z(parts, own, layer_act, out, grad, act):
    act[...] = layer_act[...]
    total = own[...]
    for j in range(1, 4):
        total += parts[lax.rem(zl_place() + j, 4), 0].astype(F32)
    out[...] = total
    grad[...] = sum_of(parts, 1)


def per_device(features, weight, adj_values, tile_rows, tile_cols, cotangent):
    adj = adj_values.reshape(16, T, T)
    rows = tile_rows.reshape(16)
    cols = tile_cols.reshape(16)
    tile = (T, F)

    (own,) = call(copies, [((4, T, F), BF)], "v")(features)
    own = exchange(own, "zl")
    own = exchange(jnp.broadcast_to(own[None], (4, 4, T, F)), "x").reshape(16, T, F)
    other = swap_core(own)
    partial, mine = call(
        forward_tiles,
        [((4, 4, T, F), BF), ((4, T, F), F32)],
        "ssvvv",
        [pltpu.VMEM((16, T, F), F32)] * 2,
    )(rows, cols, adj, own, other)
    parts = exchange(partial, "y")
    (summed,) = call(add_y, [((5, T, F), BF)], "vvv")(parts, mine, cotangent)
    parts = gather(summed, "zh")
    act, back = call(
        layer, [(tile, F32), ((4, 6, T, F), BF)], "vv", [pltpu.VMEM((4, T, F), F32)]
    )(parts, weight)
    parts = exchange(back, "y")
    keeps, grad, send = call(
        backward_tiles,
        [((2, 16, T, F), F32), (tile, F32), ((18, T, F), BF)],
        "ssvv",
        [pltpu.VMEM((16, T, F), F32)],
    )(rows, cols, adj, parts)
    got = swap_core(send)
    parts, mine = call(add_cores, [((4, 5, T, F), BF), ((4, T, F), F32)], "vvv")(keeps, grad, got)
    parts = exchange(parts, "x")
    parts, own = call(
        add_x, [((4, 2, T, F), BF), (tile, F32)], "vv", [pltpu.VMEM((4, T, F), F32)]
    )(parts, mine)
    parts = exchange(parts, "zl")
    out, grad, act = call(add_z, [(tile, F32)] * 3, "vvv")(parts, own, act)
    return act, out, grad


def solution(mesh):
    return jax.shard_map(
        per_device,
        mesh=mesh,
        in_specs=(
            P(BOTH, None),
            P(),
            P("row", "col", None, None, None),
            P("row", "col", None),
            P("row", "col", None),
            P(BOTH, None),
        ),
        out_specs=(P(BOTH, None), P(BOTH, None), P()),
        check_vma=False,
    )
```

```python
import itertools

import jax
import jax.numpy as jnp
from jax import lax
from jax.experimental import pallas as pl
from jax.experimental.pallas import tpu as pltpu
from jax.sharding import PartitionSpec as P

BOTH = ("row", "col")
SIZES = {"x": 4, "zl": 4, "core": 2, "y": 4, "zh": 4}
F = 128
T = 128
BF = jnp.bfloat16
F32 = jnp.float32


def position(place):
    n = 0
    for name, size in SIZES.items():
        n = n * size + place[name]
    return n


def places():
    for values in itertools.product(*(range(s) for s in SIZES.values())):
        yield dict(zip(SIZES, values))


def groups(axis, turned=False):
    found = {}
    for place in places():
        key = tuple(v for n, v in place.items() if n != axis)
        found.setdefault(key, []).append(place)
    return [
        [position(p) for p in (g[::-1] if turned and g[0]["core"] else g)]
        for g in found.values()
    ]


def swap_core(array):
    pairs = [(position(p), position({**p, "core": 1 - p["core"]})) for p in places()]
    return lax.ppermute(array, BOTH, pairs)


def gather(array, axis):
    return lax.all_gather(array, BOTH, axis=0, tiled=False, axis_index_groups=groups(axis))


def exchange(array, axis, turned=False):
    members = groups(axis, turned)
    return lax.all_to_all(array, BOTH, 0, 0, tiled=True, axis_index_groups=members)


def core_place():
    return lax.rem(lax.axis_index("row"), 2)


def zl_place():
    return lax.rem(lax.div(lax.axis_index("row"), 2), 4)


def x_place():
    return lax.div(lax.axis_index("row"), 8)


def zh_place():
    return lax.rem(lax.axis_index("col"), 4)


def y_place():
    return lax.div(lax.axis_index("col"), 4)


def dot(a, b, dims):
    return lax.dot_general(a, b, (dims, ((), ())), preferred_element_type=F32)


def copies(source, out):
    for k in range(4):
        out[k] = source[...]


def call(body, outs, spaces, scratch=()):
    kinds = {"v": pltpu.VMEM, "s": pltpu.SMEM}
    return pl.pallas_call(
        body,
        out_shape=[jax.ShapeDtypeStruct(s, d) for s, d in outs],
        in_specs=[pl.BlockSpec(memory_space=kinds[k]) for k in spaces],
        out_specs=[pl.BlockSpec(memory_space=pltpu.VMEM) for _ in outs],
        scratch_shapes=list(scratch),
        compiler_params=pltpu.CompilerParams(vmem_limit_bytes=16 << 20),
    )


def split(grad):
    high = grad.astype(BF)
    return high, (grad - high.astype(F32)).astype(BF)


def slot(place):
    return place + core_place() * (3 - 2 * place)


def plus_others(own, parts, place, count):
    for j in range(1, 4):
        own += parts[lax.rem(place + j, 4), pl.ds(0, count)].astype(F32)
    return own


def forward_tiles(rows, cols, adj, own, other, out, mine, acc):
    acc[...] = jnp.zeros_like(acc)
    for t in range(16):
        b = cols[t]
        spot = lax.div(b, 2)
        x = jnp.where(lax.rem(b, 2) == core_place(), own[spot], other[spot])
        r = rows[t]
        acc[r] += dot(adj[t], x, ((1,), (0,)))
    out[...] = acc[...].astype(BF).reshape(4, 4, T, F)
    mine[...] = acc[pl.ds(y_place() * 4, 4)]


def add_y(parts, mine, cot, out):
    out[pl.ds(0, 4)] = plus_others(mine[...], parts, y_place(), 4).astype(BF)
    out[4] = cot[...]


def layer(parts, weight, act, out, kept):
    total = parts[0, pl.ds(0, 4)].astype(F32)
    for k in range(1, 4):
        total += parts[k, pl.ds(0, 4)].astype(F32)
    zed, zed_low = split(total.reshape(512, F))
    w = weight[...]
    pre = dot(zed, w, ((1,), (0,))) + dot(zed_low, w, ((1,), (0,)))
    sig = jax.nn.sigmoid(pre)
    kept[...] = (pre * sig).reshape(4, T, F)
    act[...] = kept[zh_place()]
    cot = jnp.concatenate([parts[k, 4] for k in range(4)], axis=0)
    dpre, dpre_low = split(cot.astype(F32) * sig * (1.0 + pre * (1.0 - sig)))
    back = dot(dpre, w, ((1,), (1,))) + dot(dpre_low, w, ((1,), (1,)))
    back = back.astype(BF).reshape(4, T, F)
    rows = ((0,), (0,))
    grad = dot(zed, dpre, rows) + dot(zed_low, dpre, rows) + dot(zed, dpre_low, rows)
    high, low = split(grad)
    for k in range(4):
        out[k, pl.ds(0, 4)] = back
        out[k, 4] = high
        out[k, 5] = low


def backward_tiles(rows, cols, adj, parts, acc, grad, send):
    core = core_place()
    acc[...] = jnp.zeros_like(acc)
    for t in range(16):
        r = rows[t]
        b = cols[t]
        d = parts[lax.div(r, 4), lax.rem(r, 4)]
        acc[lax.rem(b, 2), lax.div(b, 2)] += dot(adj[t], d, ((0,), (0,)))
    high, low = split(sum_of(parts, 4) + sum_of(parts, 5))
    send[pl.ds(0, 16)] = acc[1 - core].astype(BF)
    grad[...] = high.astype(F32) + low.astype(F32)
    send[16] = high
    send[17] = low


def add_cores(keeps, kept_grad, got, out, mine):
    keep = keeps.at[core_place()]
    grad = (kept_grad[...] + (got[16].astype(F32) + got[17].astype(F32))).astype(BF)
    for k in range(4):
        total = keep[pl.ds(4 * k, 4)] + got[pl.ds(4 * k, 4)].astype(F32)
        out[slot(k), pl.ds(0, 4)] = total.astype(BF)
        out[k, 4] = grad
    start = x_place() * 4
    mine[...] = keep[pl.ds(start, 4)] + got[pl.ds(start, 4)].astype(F32)


def sum_of(parts, spot):
    one, two, three, four = (parts[k, spot].astype(F32) for k in range(4))
    return (one + four) + (two + three)


def add_x(parts, mine, out, own, kept):
    total = plus_others(mine[...], parts, slot(x_place()), 4)
    grad = sum_of(parts, 4).astype(BF)
    for k in range(4):
        out[slot(k), 0] = total[k].astype(BF)
        out[k, 1] = grad
    kept[...] = total
    own[...] = kept[zl_place()]


def add_z(parts, own, layer_act, out, grad, act):
    act[...] = layer_act[...]
    total = own[...]
    for j in range(1, 4):
        total += parts[lax.rem(slot(zl_place()) + j, 4), 0].astype(F32)
    out[...] = total
    grad[...] = sum_of(parts, 1)


def per_device(features, weight, adj_values, tile_rows, tile_cols, cotangent):
    adj = adj_values.reshape(16, T, T)
    rows = tile_rows.reshape(16)
    cols = tile_cols.reshape(16)
    tile = (T, F)

    (own,) = call(copies, [((4, T, F), BF)], "v")(features)
    own = exchange(own, "zl")
    own = exchange(jnp.broadcast_to(own[None], (4, 4, T, F)), "x").reshape(16, T, F)
    other = swap_core(own)
    partial, mine = call(
        forward_tiles,
        [((4, 4, T, F), BF), ((4, T, F), F32)],
        "ssvvv",
        [pltpu.VMEM((16, T, F), F32)],
    )(rows, cols, adj, own, other)
    parts = exchange(partial, "y")
    (summed,) = call(add_y, [((5, T, F), BF)], "vvv")(parts, mine, cotangent)
    parts = gather(summed, "zh")
    act, back = call(
        layer, [(tile, F32), ((4, 6, T, F), BF)], "vv", [pltpu.VMEM((4, T, F), F32)]
    )(parts, weight)
    parts = exchange(back, "y")
    keeps, grad, send = call(
        backward_tiles, [((2, 16, T, F), F32), (tile, F32), ((18, T, F), BF)], "ssvv"
    )(rows, cols, adj, parts)
    got = swap_core(send)
    parts, mine = call(add_cores, [((4, 5, T, F), BF), ((4, T, F), F32)], "vvv")(keeps, grad, got)
    parts = exchange(parts, "x", True)
    parts, own = call(
        add_x, [((4, 2, T, F), BF), (tile, F32)], "vv", [pltpu.VMEM((4, T, F), F32)]
    )(parts, mine)
    parts = exchange(parts, "zl", True)
    out, grad, act = call(add_z, [(tile, F32)] * 3, "vvv")(parts, own, act)
    return act, out, grad


def solution(mesh):
    return jax.shard_map(
        per_device,
        mesh=mesh,
        in_specs=(
            P(BOTH, None),
            P(),
            P("row", "col", None, None, None),
            P("row", "col", None),
            P("row", "col", None),
            P(BOTH, None),
        ),
        out_specs=(P(BOTH, None), P(BOTH, None), P()),
        check_vma=False,
    )
```

```python
import itertools

import jax
import jax.numpy as jnp
from jax import lax
from jax.experimental import pallas as pl
from jax.experimental.pallas import tpu as pltpu
from jax.sharding import PartitionSpec as P

BOTH = ("row", "col")
SIZES = {"x": 4, "zl": 4, "core": 2, "y": 4, "zh": 4}
F = 128
T = 128
BF = jnp.bfloat16
F32 = jnp.float32


def position(place):
    n = 0
    for name, size in SIZES.items():
        n = n * size + place[name]
    return n


def places():
    for values in itertools.product(*(range(s) for s in SIZES.values())):
        yield dict(zip(SIZES, values))


def groups(axis, turned=False):
    found = {}
    for place in places():
        key = tuple(v for n, v in place.items() if n != axis)
        found.setdefault(key, []).append(place)
    return [
        [position(p) for p in (g[::-1] if turned and g[0]["core"] else g)]
        for g in found.values()
    ]


def swap_core(array):
    pairs = [(position(p), position({**p, "core": 1 - p["core"]})) for p in places()]
    return lax.ppermute(array, BOTH, pairs)


def gather(array, axis):
    return lax.all_gather(array, BOTH, axis=0, tiled=False, axis_index_groups=groups(axis))


def exchange(array, axis, turned=False):
    members = groups(axis, turned)
    return lax.all_to_all(array, BOTH, 0, 0, tiled=True, axis_index_groups=members)


def core_place():
    return lax.rem(lax.axis_index("row"), 2)


def zl_place():
    return lax.rem(lax.div(lax.axis_index("row"), 2), 4)


def x_place():
    return lax.div(lax.axis_index("row"), 8)


def zh_place():
    return lax.rem(lax.axis_index("col"), 4)


def y_place():
    return lax.div(lax.axis_index("col"), 4)


def dot(a, b, dims):
    return lax.dot_general(a, b, (dims, ((), ())), preferred_element_type=F32)


def copies(source, out):
    for k in range(4):
        out[k] = source[...]


def call(body, outs, spaces, scratch=()):
    kinds = {"v": pltpu.VMEM, "s": pltpu.SMEM}
    return pl.pallas_call(
        body,
        out_shape=[jax.ShapeDtypeStruct(s, d) for s, d in outs],
        in_specs=[pl.BlockSpec(memory_space=kinds[k]) for k in spaces],
        out_specs=[pl.BlockSpec(memory_space=pltpu.VMEM) for _ in outs],
        scratch_shapes=list(scratch),
        compiler_params=pltpu.CompilerParams(vmem_limit_bytes=16 << 20),
    )


def split(grad):
    high = grad.astype(BF)
    return high, (grad - high.astype(F32)).astype(BF)


def slot(place):
    return place + core_place() * (3 - 2 * place)


def plus_others(own, parts, place, count):
    for j in range(1, 4):
        own += parts[lax.rem(place + j, 4), pl.ds(0, count)].astype(F32)
    return own


def forward_tiles(rows, cols, adj, own, other, out, mine, acc):
    acc[...] = jnp.zeros_like(acc)
    for t in range(16):
        b = cols[t]
        spot = lax.div(b, 2)
        x = jnp.where(lax.rem(b, 2) == core_place(), own[spot], other[spot])
        r = rows[t]
        acc[r] += dot(adj[t], x, ((1,), (0,)))
    for k in range(4):
        out[slot(k)] = acc[pl.ds(4 * k, 4)].astype(BF)
    mine[...] = acc[pl.ds(y_place() * 4, 4)]


def add_y(parts, mine, cot, out):
    out[pl.ds(0, 4)] = plus_others(mine[...], parts, slot(y_place()), 4).astype(BF)
    out[4] = cot[...]


def layer(parts, weight, act, out, kept):
    total = parts[0, pl.ds(0, 4)].astype(F32)
    for k in range(1, 4):
        total += parts[k, pl.ds(0, 4)].astype(F32)
    zed, zed_low = split(total.reshape(512, F))
    w = weight[...]
    pre = dot(zed, w, ((1,), (0,))) + dot(zed_low, w, ((1,), (0,)))
    sig = jax.nn.sigmoid(pre)
    kept[...] = (pre * sig).reshape(4, T, F)
    act[...] = kept[zh_place()]
    cot = jnp.concatenate([parts[k, 4] for k in range(4)], axis=0)
    dpre, dpre_low = split(cot.astype(F32) * sig * (1.0 + pre * (1.0 - sig)))
    back = dot(dpre, w, ((1,), (1,))) + dot(dpre_low, w, ((1,), (1,)))
    back = back.astype(BF).reshape(4, T, F)
    rows = ((0,), (0,))
    grad = dot(zed, dpre, rows) + dot(zed_low, dpre, rows) + dot(zed, dpre_low, rows)
    high, low = split(grad)
    for k in range(4):
        out[k, pl.ds(0, 4)] = back
        out[k, 4] = high
        out[k, 5] = low


def backward_tiles(rows, cols, adj, parts, acc, grad, send):
    core = core_place()
    acc[...] = jnp.zeros_like(acc)
    for t in range(16):
        r = rows[t]
        b = cols[t]
        d = parts[lax.div(r, 4), lax.rem(r, 4)]
        acc[lax.rem(b, 2), lax.div(b, 2)] += dot(adj[t], d, ((0,), (0,)))
    high, low = split(sum_of(parts, 4) + sum_of(parts, 5))
    send[pl.ds(0, 16)] = acc[1 - core].astype(BF)
    grad[...] = high.astype(F32) + low.astype(F32)
    send[16] = high
    send[17] = low


def add_cores(keeps, kept_grad, got, out, mine):
    keep = keeps.at[core_place()]
    grad = (kept_grad[...] + (got[16].astype(F32) + got[17].astype(F32))).astype(BF)
    for k in range(4):
        total = keep[pl.ds(4 * k, 4)] + got[pl.ds(4 * k, 4)].astype(F32)
        out[slot(k), pl.ds(0, 4)] = total.astype(BF)
        out[k, 4] = grad
    start = x_place() * 4
    mine[...] = keep[pl.ds(start, 4)] + got[pl.ds(start, 4)].astype(F32)


def sum_of(parts, spot):
    one, two, three, four = (parts[k, spot].astype(F32) for k in range(4))
    return (one + four) + (two + three)


def add_x(parts, mine, out, own, kept):
    total = plus_others(mine[...], parts, slot(x_place()), 4)
    grad = sum_of(parts, 4).astype(BF)
    for k in range(4):
        out[slot(k), 0] = total[k].astype(BF)
        out[k, 1] = grad
    kept[...] = total
    own[...] = kept[zl_place()]


def add_z(parts, own, layer_act, out, grad, act):
    act[...] = layer_act[...]
    total = own[...]
    for j in range(1, 4):
        total += parts[lax.rem(slot(zl_place()) + j, 4), 0].astype(F32)
    out[...] = total
    grad[...] = sum_of(parts, 1)


def per_device(features, weight, adj_values, tile_rows, tile_cols, cotangent):
    adj = adj_values.reshape(16, T, T)
    rows = tile_rows.reshape(16)
    cols = tile_cols.reshape(16)
    tile = (T, F)

    (own,) = call(copies, [((4, T, F), BF)], "v")(features)
    own = exchange(own, "zl")
    own = exchange(jnp.broadcast_to(own[None], (4, 4, T, F)), "x").reshape(16, T, F)
    other = swap_core(own)
    partial, mine = call(
        forward_tiles,
        [((4, 4, T, F), BF), ((4, T, F), F32)],
        "ssvvv",
        [pltpu.VMEM((16, T, F), F32)],
    )(rows, cols, adj, own, other)
    parts = exchange(partial, "y", True)
    (summed,) = call(add_y, [((5, T, F), BF)], "vvv")(parts, mine, cotangent)
    parts = gather(summed, "zh")
    act, back = call(
        layer, [(tile, F32), ((4, 6, T, F), BF)], "vv", [pltpu.VMEM((4, T, F), F32)]
    )(parts, weight)
    parts = exchange(back, "y")
    keeps, grad, send = call(
        backward_tiles, [((2, 16, T, F), F32), (tile, F32), ((18, T, F), BF)], "ssvv"
    )(rows, cols, adj, parts)
    got = swap_core(send)
    parts, mine = call(add_cores, [((4, 5, T, F), BF), ((4, T, F), F32)], "vvv")(keeps, grad, got)
    parts = exchange(parts, "x", True)
    parts, own = call(
        add_x, [((4, 2, T, F), BF), (tile, F32)], "vv", [pltpu.VMEM((4, T, F), F32)]
    )(parts, mine)
    parts = exchange(parts, "zl", True)
    out, grad, act = call(add_z, [(tile, F32)] * 3, "vvv")(parts, own, act)
    return act, out, grad


def solution(mesh):
    return jax.shard_map(
        per_device,
        mesh=mesh,
        in_specs=(
            P(BOTH, None),
            P(),
            P("row", "col", None, None, None),
            P("row", "col", None),
            P("row", "col", None),
            P(BOTH, None),
        ),
        out_specs=(P(BOTH, None), P(BOTH, None), P()),
        check_vma=False,
    )
```
